32 devices in a mesh: space: 16 (over z, x, core), trial: 2 (over y).
Axes of the slice: x: 2, y: 2, z: 4, core: 2. Of those that a mesh axis runs over, the one named last changes fastest.
Arguments:
- trial_x: bfloat16 [4, 4096, 1024], P('trial', 'space')
- h_panel: bfloat16 [4096, 640], P('space')
- s_panel: bfloat16 [4096, 640], P('space')
- pattern: int32 [64, 10], P('space'), may hold values from 0 to 63, as said below
Outputs:
- theta: float32 [4], P('trial')
- new_dirs: bfloat16 [4, 4096, 1024], P('trial', 'space')
- mean_sq: float32 [4], P('trial')
The draws below stay inside these ranges and needn't reach their ends.
Inputs may be any that keep to these rules, and one draw needn't show every extreme that they name: pattern[a, 0] is a; the entries of a row are distinct atoms of a's own spatial domain or of the two domains beside it (cyclically), the domain of atom a being a // 4.
All inputs are finite; a program needn't handle non-finite values.
Results may differ from the reference program's by a relative error of at most 0.0006.
Values may be sent and summed in bfloat16 or wider, within the bound.
A program may use at most 128 MiB of HBM per device.

```python
import math
import jax
import jax.numpy as jnp
from jax import lax

BLOCK = 64
SLOTS = 10
ATOM_DEV = 4
COLS = 1024
STATES = 4
ATOMS = 64
ROWS = 4096


def draw_trial_x(key, part):
    total_rows = ATOMS * BLOCK
    common = jax.random.normal(jax.random.fold_in(key, 11), (1, total_rows, COLS), jnp.float32)
    single = jax.random.normal(jax.random.fold_in(key, 12), (STATES, total_rows, COLS), jnp.float32)
    row_place = jnp.arange(total_rows).astype(jnp.float32) / (total_rows - 1)
    row_spread = jnp.exp(jax.random.uniform(jax.random.fold_in(key, 13), (total_rows,), jnp.float32, 0.0, math.log(3.3)))
    col_spread = jnp.exp(jax.random.uniform(jax.random.fold_in(key, 14), (COLS,), jnp.float32, 0.0, math.log(10.0)))
    shared_part = 0.6
    single_part = 0.8
    rising = jnp.exp(math.log(10.0) * row_place)
    values = (shared_part * common + single_part * single) * (rising * row_spread)[None, :, None] * col_spread[None, None, :]
    return values.astype(jnp.bfloat16)


def tile_draw(key, onsite, off_scale):
    total_rows = ATOMS * BLOCK
    shape = (total_rows, SLOTS * BLOCK)
    spread = off_scale / math.sqrt(SLOTS * BLOCK)
    coupling = jax.random.normal(jax.random.fold_in(key, 21), shape, jnp.float32) * spread
    row_index = jnp.arange(total_rows)[:, None]
    col_index = jnp.arange(SLOTS * BLOCK)[None, :]
    on_diagonal = jnp.logical_and(col_index < BLOCK, col_index == row_index % BLOCK)
    return coupling + jnp.where(on_diagonal, onsite, 0.0)


def draw_h_panel(key, part):
    energies = jax.random.uniform(jax.random.fold_in(key, 31), (ATOMS * BLOCK, 1), jnp.float32, 0.5, 4.0)
    return tile_draw(key, energies, 1.0).astype(jnp.bfloat16)


def draw_s_panel(key, part):
    return tile_draw(jax.random.fold_in(key, 41), jnp.ones((ATOMS * BLOCK, 1), jnp.float32), 0.7).astype(jnp.bfloat16)


def draw_pattern(key, part):
    keys = jax.random.split(jax.random.fold_in(key, 51), ATOMS)
    shuffled = jax.vmap(lambda one_key: jax.random.permutation(one_key, 3 * ATOM_DEV - 1))(keys)
    chosen = shuffled[:, :SLOTS - 1].astype(jnp.int32)
    atom_ids = jnp.arange(ATOMS, dtype=jnp.int32)
    own_place = ATOM_DEV + atom_ids % ATOM_DEV
    places = chosen + (chosen >= own_place[:, None]).astype(jnp.int32)
    first_atom = atom_ids - atom_ids % ATOM_DEV - ATOM_DEV
    neighbours = jnp.mod(first_atom[:, None] + places, ATOMS).astype(jnp.int32)
    return jnp.concatenate([atom_ids[:, None], neighbours], axis=1).astype(jnp.int32)


def setup_inputs(seed: int = 0) -> dict:
    key_list = jax.random.split(jax.random.key(seed), 5)
    return {
        "trial_x": draw_trial_x(jax.random.fold_in(key_list[4], 71), 0),
        "h_panel": draw_h_panel(jax.random.fold_in(key_list[4], 71), 0),
        "s_panel": draw_s_panel(jax.random.fold_in(key_list[4], 71), 0),
        "pattern": draw_pattern(jax.random.fold_in(key_list[4], 71), 0),
    }


def reference(trial_x, h_panel, s_panel, pattern):
    blocks = trial_x.reshape(STATES, ATOMS, BLOCK, COLS)
    h_tiles = h_panel.astype(jnp.float32).reshape(ATOMS, BLOCK, SLOTS, BLOCK)
    s_tiles = s_panel.astype(jnp.float32).reshape(ATOMS, BLOCK, SLOTS, BLOCK)

    def apply_state(state_blocks):
        picked = state_blocks[pattern].astype(jnp.float32)
        h_image = jnp.einsum('apbq,abqw->apw', h_tiles, picked, precision=lax.Precision.HIGHEST)
        s_image = jnp.einsum('apbq,abqw->apw', s_tiles, picked, precision=lax.Precision.HIGHEST)
        return (h_image.reshape(ROWS * COLS), s_image.reshape(ROWS * COLS))
    flat_h, flat_s = lax.map(apply_state, blocks)
    cross = lax.optimization_barrier(jnp.sum(flat_s * flat_h, axis=1))
    weight = lax.optimization_barrier(jnp.sum(flat_s * flat_s, axis=1))
    theta = cross / (weight + 1e-06)
    flat_r = flat_h - theta[:, None] * flat_s
    flat_x = trial_x.reshape(STATES, ROWS * COLS)
    gram = jnp.dot(flat_x.astype(jnp.float32), flat_x.T.astype(jnp.float32), preferred_element_type=jnp.float32)
    wide_x = flat_x.astype(jnp.float32)
    correlation = jnp.dot(wide_x, flat_r.T, precision=lax.Precision.HIGHEST)
    factor = jnp.linalg.cholesky(gram)
    coeffs = jax.scipy.linalg.cho_solve((factor, True), correlation)
    normal_part = flat_r - jnp.dot(coeffs.T, wide_x, precision=lax.Precision.HIGHEST)
    mean_sq = lax.optimization_barrier(jnp.sum(normal_part * normal_part, axis=1)) / (ROWS * COLS)
    scaled = normal_part * lax.rsqrt(mean_sq + 1e-06)[:, None]
    new_dirs = scaled.astype(jnp.bfloat16).reshape(STATES, ROWS, COLS)
    return (theta, new_dirs, mean_sq)
```

```python
import functools

import jax
import jax.numpy as jnp
from jax import lax
from jax.experimental import pallas as pl
from jax.experimental.pallas import tpu as pltpu
from jax.sharding import PartitionSpec as P

F32, BF16 = jnp.float32, jnp.bfloat16
GROUP = 30


def stat_pairs(own, states):
    pairs = [(("s", k), ("h", k)) for k in range(own)]
    pairs += [(("s", k), ("s", k)) for k in range(own)]
    pairs += [(("x", t), ("h", k)) for t in range(states) for k in range(own)]
    pairs += [(("x", t), ("s", k)) for t in range(states) for k in range(own)]
    pairs += [(("x", t), ("x", u)) for t in range(states) for u in range(t + 1)]
    return pairs


def cholesky_solve(gram, rhs):
    n = len(rhs)
    low = [[None] * n for _ in range(n)]
    inv = [None] * n
    for j in range(n):
        d = gram[j][j]
        for k in range(j):
            d = d - low[j][k] * low[j][k]
        inv[j] = 1.0 / jnp.sqrt(d)
        for i in range(j + 1, n):
            v = gram[i][j]
            for k in range(j):
                v = v - low[i][k] * low[j][k]
            low[i][j] = v * inv[j]
    out = []
    for col in range(len(rhs[0])):
        y = []
        for i in range(n):
            v = rhs[i][col]
            for k in range(i):
                v = v - low[i][k] * y[k]
            y.append(v * inv[i])
        z = [None] * n
        for i in reversed(range(n)):
            v = y[i]
            for k in range(i + 1, n):
                v = v - low[k][i] * z[k]
            z[i] = v * inv[i]
        out.append(z)
    return out


def body(domains, groups, chunk, pat, x, h, s, out, theta_o, msq_o,
         ext, oth, hp, sp, pick, hext, img, acc, slots, nslots, obuf,
         lsem, osem, nb_send, nb_recv, tr_send, tr_recv, st_send, st_recv, nm_send, nm_recv):
    own, rows, width = x.shape
    atoms_dev, nslot = pat.shape
    block = rows // atoms_dev
    atoms = atoms_dev * domains
    span = 3 * rows
    states = own * groups
    chunks = width // chunk
    me, mt = lax.axis_index("space"), lax.axis_index("trial")
    right, left = lax.rem(me + 1, domains), lax.rem(me + domains - 1, domains)

    loads = [
        pltpu.make_async_copy(x, ext.at[:, pl.ds(rows, rows), :], lsem.at[0]),
        pltpu.make_async_copy(h, hp, lsem.at[1]),
        pltpu.make_async_copy(s, sp, lsem.at[2]),
    ]
    for load in loads:
        load.start()

    barrier = pltpu.get_barrier_semaphore()

    def greet(k, carry):
        pl.semaphore_signal(barrier, inc=1, device_id={"space": lax.rem(me + k, domains)})
        return carry
    lax.fori_loop(1, domains, greet, 0)
    for k in range(1, groups):
        pl.semaphore_signal(barrier, inc=1, device_id={"trial": lax.rem(mt + k, groups)})
    pl.semaphore_wait(barrier, domains - 1 + groups - 1)

    def neighbour_copy(side, c):
        cols = pl.ds(pl.multiple_of(c * chunk, chunk), chunk)
        return pltpu.make_async_remote_copy(
            src_ref=x.at[:, :, cols],
            dst_ref=ext.at[:, pl.ds(2 * rows * side, rows), cols],
            send_sem=nb_send.at[side, c], recv_sem=nb_recv.at[side, c],
            device_id={"space": left if side else right})

    def trial_copy(k, c):
        cols = pl.ds(pl.multiple_of(c * chunk, chunk), chunk)
        return pltpu.make_async_remote_copy(
            src_ref=x.at[:, :, cols], dst_ref=oth.at[k - 1, :, :, cols],
            send_sem=tr_send.at[k - 1, c], recv_sem=tr_recv.at[k - 1, c],
            device_id={"trial": lax.rem(mt + k, groups)})

    def arrivals(c):
        return [neighbour_copy(0, c), neighbour_copy(1, c)] + [trial_copy(k, c) for k in range(1, groups)]

    for c in range(chunks):
        for copy in arrivals(c):
            copy.start()

    acc[...] = jnp.zeros_like(acc)
    loads[1].wait()
    loads[2].wait()
    diff = (lax.broadcasted_iota(jnp.int32, (block, span), 1)
            - lax.broadcasted_iota(jnp.int32, (block, span), 0))

    def densify(a, carry):
        for b in range(nslot):
            link = lax.rem(pat[a, b] - me * atoms_dev + atoms_dev + atoms, atoms)
            pick[b * block:(b + 1) * block, :] = jnp.where(diff == link * block, 1.0, 0.0).astype(BF16)
        at = pl.multiple_of(a * block, block)
        ha = jnp.dot(hp[pl.ds(at, block), :], pick[...], preferred_element_type=F32)
        hext[pl.ds(at, block), :] = ha.astype(BF16)
        sa = jnp.dot(sp[pl.ds(at, block), :], pick[...], preferred_element_type=F32)
        hext[pl.ds(pl.multiple_of(rows + a * block, block), block), :] = sa.astype(BF16)
        return carry
    lax.fori_loop(0, atoms_dev, densify, 0)
    loads[0].wait()

    pairs = stat_pairs(own, states)

    def fetch(name, at, col):
        kind, k = name
        cols = pl.ds(pl.multiple_of(col, 128), 128)
        if kind == "h":
            return img[k, pl.ds(at, 16), cols]
        if kind == "s":
            return img[k, pl.ds(pl.multiple_of(rows + at, 16), 16), cols]
        if k < own:
            return ext[k, pl.ds(pl.multiple_of(rows + at, 16), 16), cols].astype(F32)
        return oth[k // own - 1, k % own, pl.ds(at, 16), cols].astype(F32)

    def on_chunk(c, carry):
        for copy in arrivals(c):
            copy.wait_recv()
        cols = pl.ds(pl.multiple_of(c * chunk, chunk), chunk)
        for k in range(own):
            img[k, :, cols] = jnp.dot(hext[...], ext[k, :, cols], preferred_element_type=F32)
        for first in range(0, len(pairs), GROUP):
            part = pairs[first:first + GROUP]

            def on_rows(r, sums):
                at = pl.multiple_of(r * 16, 16)
                for piece in range(chunk // 128):
                    have = {}
                    new = []
                    for (a, b), total in zip(part, sums):
                        for name in (a, b):
                            if name not in have:
                                have[name] = fetch(name, at, c * chunk + piece * 128)
                        p = have[a] * have[b]
                        new.append(total + (p[:8] + p[8:]))
                    sums = tuple(new)
                return sums
            zero = jnp.zeros((8, 128), F32)
            sums = lax.fori_loop(0, rows // 16, on_rows, (zero,) * len(part))
            for i, v in enumerate(sums):
                acc[first + i] += v
        return carry
    lax.fori_loop(0, chunks, on_chunk, 0)

    lane = lax.broadcasted_iota(jnp.int32, (8, 128), 1)
    message = jnp.zeros((8, 128), F32)
    for g in range(acc.shape[0] // 8):
        lines = jnp.sum(acc[g * 8:(g + 1) * 8], axis=1)
        ends = jnp.sum(lines, axis=1, keepdims=True)
        message = jnp.where(lane == g, jnp.broadcast_to(ends, (8, 128)), message)

    def share(buffer, send, recv):
        def copy(k):
            return pltpu.make_async_remote_copy(
                src_ref=buffer.at[me], dst_ref=buffer.at[me],
                send_sem=send.at[k], recv_sem=recv.at[me],
                device_id={"space": lax.rem(me + k, domains)})

        def go(k, carry):
            copy(k).start()
            return carry
        lax.fori_loop(1, domains, go, 0)

        def come(k, carry):
            peer = lax.rem(me + k, domains)
            pltpu.make_async_remote_copy(
                src_ref=buffer.at[peer], dst_ref=buffer.at[peer],
                send_sem=send.at[k], recv_sem=recv.at[peer],
                device_id={"space": peer}).wait_recv()
            return carry
        lax.fori_loop(1, domains, come, 0)

        def left_here(k, carry):
            copy(k).wait_send()
            return carry
        return lambda: lax.fori_loop(1, domains, left_here, 0)

    slots[me] = message
    end_stats = share(slots, st_send, st_recv)
    total = slots[0]
    for d in range(1, domains):
        total = total + slots[d]
    value = {}
    for i, name in enumerate(pairs):
        value[name] = jnp.broadcast_to(total[i % 8:i % 8 + 1, i // 8:i // 8 + 1], (8, 128))
    theta = [value[("s", k), ("h", k)] / (value[("s", k), ("s", k)] + 1e-06) for k in range(own)]
    corr = [[value[("x", t), ("h", k)] - theta[k] * value[("x", t), ("s", k)] for k in range(own)]
            for t in range(states)]
    gram = [[value[("x", t), ("x", u)] for u in range(t + 1)] for t in range(states)]
    coeffs = cholesky_solve(gram, corr)
    for k in range(own):
        theta_o[k] = theta[k][0, 0]

    def wide(v):
        return jnp.concatenate([v, v], axis=0)

    zero = jnp.zeros((8, 128), F32)

    def on_normal(r, sums):
        at = pl.multiple_of(r * 16, 16)
        sums = list(sums)
        for col in range(0, width, 128):
            xs = [fetch(("x", t), at, col) for t in range(states)]
            for k in range(own):
                n = fetch(("h", k), at, col) - wide(theta[k]) * fetch(("s", k), at, col)
                lump = wide(coeffs[k][0]) * xs[0]
                for t in range(1, states):
                    lump = lump + wide(coeffs[k][t]) * xs[t]
                n = n - lump
                img[k, pl.ds(at, 16), pl.ds(col, 128)] = n
                p = n * n
                sums[k] = sums[k] + (p[:8] + p[8:])
        return tuple(sums)
    sums = lax.fori_loop(0, rows // 16, on_normal, (zero,) * own)
    for k in range(own):
        nslots[me, k] = sums[k]
    end_norms = share(nslots, nm_send, nm_recv)
    scale = []
    for k in range(own):
        v = nslots[0, k]
        for d in range(1, domains):
            v = v + nslots[d, k]
        v = jnp.sum(jnp.sum(v, axis=0, keepdims=True), axis=1, keepdims=True)
        mean = jnp.broadcast_to(v, (8, 128)) / float(domains * rows * width)
        msq_o[k] = mean[0, 0]
        scale.append(wide(lax.rsqrt(mean + 1e-06)))
    stores = []
    for k in range(own):
        def on_scale(r, carry):
            at = pl.multiple_of(r * 16, 16)
            for col in range(0, width, 128):
                v = img[k, pl.ds(at, 16), pl.ds(col, 128)] * scale[k]
                obuf[k, pl.ds(at, 16), pl.ds(col, 128)] = v.astype(BF16)
            return carry
        lax.fori_loop(0, rows // 16, on_scale, 0)
        store = pltpu.make_async_copy(obuf.at[k], out.at[k], osem.at[k])
        store.start()
        stores.append(store)
    for c in range(chunks):
        for copy in arrivals(c):
            copy.wait_send()
    end_stats()
    end_norms()
    for store in stores:
        store.wait()


def on_device(domains, groups, trial_x, h_panel, s_panel, pattern):
    own, rows, width = trial_x.shape
    depth = h_panel.shape[1]
    chunk = 256
    chunks = width // chunk
    stats = -(-len(stat_pairs(own, own * groups)) // 8) * 8
    dma = pltpu.SemaphoreType.DMA
    new_dirs, theta, mean_sq = pl.pallas_call(
        functools.partial(body, domains, groups, chunk),
        out_shape=(jax.ShapeDtypeStruct(trial_x.shape, BF16),
                   jax.ShapeDtypeStruct((own,), F32), jax.ShapeDtypeStruct((own,), F32)),
        in_specs=[pl.BlockSpec(memory_space=pltpu.SMEM)] + [pl.BlockSpec(memory_space=pl.ANY)] * 3,
        out_specs=(pl.BlockSpec(memory_space=pl.ANY), pl.BlockSpec(memory_space=pltpu.SMEM),
                   pl.BlockSpec(memory_space=pltpu.SMEM)),
        scratch_shapes=[
            pltpu.VMEM((own, 3 * rows, width), BF16),
            pltpu.VMEM((groups - 1, own, rows, width), BF16),
            pltpu.VMEM((rows, depth), BF16),
            pltpu.VMEM((rows, depth), BF16),
            pltpu.VMEM((depth, 3 * rows), BF16),
            pltpu.VMEM((2 * rows, 3 * rows), BF16),
            pltpu.VMEM((own, 2 * rows, width), F32),
            pltpu.VMEM((stats, 8, 128), F32),
            pltpu.VMEM((domains, 8, 128), F32),
            pltpu.VMEM((domains, own, 8, 128), F32),
            pltpu.VMEM((own, rows, width), BF16),
            dma((3,)), dma((own,)),
            dma((2, chunks)), dma((2, chunks)),
            dma((groups - 1, chunks)), dma((groups - 1, chunks)),
            dma((domains,)), dma((domains,)), dma((domains,)), dma((domains,)),
        ],
        compiler_params=pltpu.CompilerParams(
            collective_id=0, has_side_effects=True, vmem_limit_bytes=40 * 1024 * 1024),
    )(pattern, trial_x, h_panel, s_panel)
    return theta, new_dirs, mean_sq


def solution(mesh):
    in_specs = (P("trial", "space", None), P("space", None), P("space", None), P("space", None))
    out_specs = (P("trial"), P("trial", "space", None), P("trial"))
    return jax.shard_map(
        functools.partial(on_device, mesh.shape["space"], mesh.shape["trial"]),
        mesh=mesh, in_specs=in_specs, out_specs=out_specs, check_vma=False
    )
```

```python
import functools

import jax
import jax.numpy as jnp
from jax import lax
from jax.experimental import pallas as pl
from jax.experimental.pallas import tpu as pltpu
from jax.sharding import PartitionSpec as P

F32, BF16 = jnp.float32, jnp.bfloat16
GROUP = 30


def stat_pairs(own, states):
    pairs = [(("s", k), ("h", k)) for k in range(own)]
    pairs += [(("s", k), ("s", k)) for k in range(own)]
    pairs += [(("x", t), ("h", k)) for t in range(states) for k in range(own)]
    pairs += [(("x", t), ("s", k)) for t in range(states) for k in range(own)]
    pairs += [(("x", t), ("x", u)) for t in range(states) for u in range(t + 1)]
    return pairs


def cholesky_solve(gram, rhs):
    n = len(rhs)
    low = [[None] * n for _ in range(n)]
    inv = [None] * n
    for j in range(n):
        d = gram[j][j]
        for k in range(j):
            d = d - low[j][k] * low[j][k]
        inv[j] = 1.0 / jnp.sqrt(d)
        for i in range(j + 1, n):
            v = gram[i][j]
            for k in range(j):
                v = v - low[i][k] * low[j][k]
            low[i][j] = v * inv[j]
    out = []
    for col in range(len(rhs[0])):
        y = []
        for i in range(n):
            v = rhs[i][col]
            for k in range(i):
                v = v - low[i][k] * y[k]
            y.append(v * inv[i])
        z = [None] * n
        for i in reversed(range(n)):
            v = y[i]
            for k in range(i + 1, n):
                v = v - low[k][i] * z[k]
            z[i] = v * inv[i]
        out.append(z)
    return out


def body(domains, groups, chunk, pat_hbm, x, h, s, out, facts,
         pat, ext, oth, hp, sp, pick, hext, img, acc, slots, nslots,
         lsem, nb_send, nb_recv, tr_send, tr_recv, st_send, st_recv, nm_send, nm_recv):
    own, rows, width = x.shape
    atoms_dev, nslot = pat.shape
    block = rows // atoms_dev
    atoms = atoms_dev * domains
    span = 3 * rows
    states = own * groups
    chunks = width // chunk
    me, mt = lax.axis_index("space"), lax.axis_index("trial")
    right, left = lax.rem(me + 1, domains), lax.rem(me + domains - 1, domains)

    loads = [
        pltpu.make_async_copy(x, ext.at[:, pl.ds(rows, rows), :], lsem.at[0]),
        pltpu.make_async_copy(h, hp, lsem.at[1]),
        pltpu.make_async_copy(s, sp, lsem.at[2]),
        pltpu.make_async_copy(pat_hbm, pat, lsem.at[3]),
    ]
    for load in loads:
        load.start()

    barrier = pltpu.get_barrier_semaphore()

    def greet(k, carry):
        pl.semaphore_signal(barrier, inc=1, device_id={"space": lax.rem(me + k, domains)})
        return carry
    lax.fori_loop(1, domains, greet, 0)
    for k in range(1, groups):
        pl.semaphore_signal(barrier, inc=1, device_id={"trial": lax.rem(mt + k, groups)})
    pl.semaphore_wait(barrier, domains - 1 + groups - 1)

    def neighbour_copy(side, c):
        cols = pl.ds(pl.multiple_of(c * chunk, chunk), chunk)
        return pltpu.make_async_remote_copy(
            src_ref=x.at[:, :, cols],
            dst_ref=ext.at[:, pl.ds(2 * rows * side, rows), cols],
            send_sem=nb_send.at[side, c], recv_sem=nb_recv.at[side, c],
            device_id={"space": left if side else right})

    def trial_copy(k, c):
        cols = pl.ds(pl.multiple_of(c * chunk, chunk), chunk)
        return pltpu.make_async_remote_copy(
            src_ref=x.at[:, :, cols], dst_ref=oth.at[k - 1, :, :, cols],
            send_sem=tr_send.at[k - 1, c], recv_sem=tr_recv.at[k - 1, c],
            device_id={"trial": lax.rem(mt + k, groups)})

    def arrivals(c):
        return [neighbour_copy(0, c), neighbour_copy(1, c)] + [trial_copy(k, c) for k in range(1, groups)]

    for c in range(chunks):
        for copy in arrivals(c):
            copy.start()

    acc[...] = jnp.zeros_like(acc)
    loads[1].wait()
    loads[2].wait()
    loads[3].wait()
    diff = (lax.broadcasted_iota(jnp.int32, (block, span), 1)
            - lax.broadcasted_iota(jnp.int32, (block, span), 0))

    def densify(a, carry):
        for b in range(nslot):
            link = lax.rem(pat[a, b] - me * atoms_dev + atoms_dev + atoms, atoms)
            pick[b * block:(b + 1) * block, :] = jnp.where(diff == link * block, 1.0, 0.0).astype(BF16)
        at = pl.multiple_of(a * block, block)
        ha = jnp.dot(hp[pl.ds(at, block), :], pick[...], preferred_element_type=F32)
        hext[pl.ds(at, block), :] = ha.astype(BF16)
        sa = jnp.dot(sp[pl.ds(at, block), :], pick[...], preferred_element_type=F32)
        hext[pl.ds(pl.multiple_of(rows + a * block, block), block), :] = sa.astype(BF16)
        return carry
    lax.fori_loop(0, atoms_dev, densify, 0)
    loads[0].wait()

    pairs = stat_pairs(own, states)

    def fetch(name, at, col):
        kind, k = name
        cols = pl.ds(pl.multiple_of(col, 128), 128)
        if kind == "h":
            return img[k, pl.ds(at, 16), cols]
        if kind == "s":
            return img[k, pl.ds(pl.multiple_of(rows + at, 16), 16), cols]
        if k < own:
            return ext[k, pl.ds(pl.multiple_of(rows + at, 16), 16), cols].astype(F32)
        return oth[k // own - 1, k % own, pl.ds(at, 16), cols].astype(F32)

    def on_chunk(c, carry):
        for copy in arrivals(c):
            copy.wait_recv()
        cols = pl.ds(pl.multiple_of(c * chunk, chunk), chunk)
        for k in range(own):
            img[k, :, cols] = jnp.dot(hext[...], ext[k, :, cols], preferred_element_type=F32)
        for first in range(0, len(pairs), GROUP):
            part = pairs[first:first + GROUP]

            def on_rows(r, sums):
                at = pl.multiple_of(r * 16, 16)
                for piece in range(chunk // 128):
                    have = {}
                    new = []
                    for (a, b), total in zip(part, sums):
                        for name in (a, b):
                            if name not in have:
                                have[name] = fetch(name, at, c * chunk + piece * 128)
                        p = have[a] * have[b]
                        new.append(total + (p[:8] + p[8:]))
                    sums = tuple(new)
                return sums
            zero = jnp.zeros((8, 128), F32)
            sums = lax.fori_loop(0, rows // 16, on_rows, (zero,) * len(part))
            for i, v in enumerate(sums):
                acc[first + i] += v
        return carry
    lax.fori_loop(0, chunks, on_chunk, 0)

    lines = slots.shape[1]
    spot = (lax.broadcasted_iota(jnp.int32, (8, 128), 1)
            - lax.broadcasted_iota(jnp.int32, (8, 128), 0))
    for line in range(lines):
        message = jnp.zeros((8, 128), F32)
        for g in range(16 * line, min(16 * line + 16, acc.shape[0] // 8)):
            ends = jnp.sum(jnp.sum(acc[g * 8:(g + 1) * 8], axis=1), axis=1, keepdims=True)
            message = jnp.where(spot == (g % 16) * 8, jnp.broadcast_to(ends, (8, 128)), message)
        slots[me, line:line + 1] = jnp.sum(message, axis=0, keepdims=True)

    def share(buffer, send, recv):
        def copy(k):
            return pltpu.make_async_remote_copy(
                src_ref=buffer.at[me], dst_ref=buffer.at[me],
                send_sem=send.at[k], recv_sem=recv.at[me],
                device_id={"space": lax.rem(me + k, domains)})

        def go(k, carry):
            copy(k).start()
            return carry
        lax.fori_loop(1, domains, go, 0)

        def come(k, carry):
            peer = lax.rem(me + k, domains)
            pltpu.make_async_remote_copy(
                src_ref=buffer.at[peer], dst_ref=buffer.at[peer],
                send_sem=send.at[k], recv_sem=recv.at[peer],
                device_id={"space": peer}).wait_recv()
            return carry
        lax.fori_loop(1, domains, come, 0)

        def left_here(k, carry):
            copy(k).wait_send()
            return carry
        return lambda: lax.fori_loop(1, domains, left_here, 0)

    end_stats = share(slots, st_send, st_recv)
    total = slots[0]
    for d in range(1, domains):
        total = total + slots[d]
    value = {}
    for i, name in enumerate(pairs):
        value[name] = jnp.broadcast_to(total[i // 128:i // 128 + 1, i % 128:i % 128 + 1], (8, 128))
    theta = [value[("s", k), ("h", k)] / (value[("s", k), ("s", k)] + 1e-06) for k in range(own)]
    corr = [[value[("x", t), ("h", k)] - theta[k] * value[("x", t), ("s", k)] for k in range(own)]
            for t in range(states)]
    gram = [[value[("x", t), ("x", u)] for u in range(t + 1)] for t in range(states)]
    coeffs = cholesky_solve(gram, corr)
    for k in range(own):
        facts[k] = theta[k][0, 0]

    def wide(v):
        return jnp.concatenate([v, v], axis=0)

    zero = jnp.zeros((8, 128), F32)

    def on_normal(r, sums):
        at = pl.multiple_of(r * 16, 16)
        sums = list(sums)
        for col in range(0, width, 128):
            xs = [fetch(("x", t), at, col) for t in range(states)]
            for k in range(own):
                n = fetch(("h", k), at, col) - wide(theta[k]) * fetch(("s", k), at, col)
                lump = wide(coeffs[k][0]) * xs[0]
                for t in range(1, states):
                    lump = lump + wide(coeffs[k][t]) * xs[t]
                n = n - lump
                out[k, pl.ds(at, 16), pl.ds(col, 128)] = n
                p = n * n
                sums[k] = sums[k] + (p[:8] + p[8:])
        return tuple(sums)
    sums = lax.fori_loop(0, rows // 16, on_normal, (zero,) * own)
    for k in range(own):
        nslots[me, k:k + 1] = jnp.sum(sums[k], axis=0, keepdims=True)
    end_norms = share(nslots, nm_send, nm_recv)
    norm = nslots[0]
    for d in range(1, domains):
        norm = norm + nslots[d]
    norm = jnp.sum(norm, axis=1, keepdims=True) / float(domains * rows * width)
    for k in range(own):
        facts[own + k] = norm[k, 0]
    for c in range(chunks):
        for copy in arrivals(c):
            copy.wait_send()
    end_stats()
    end_norms()


def on_device(domains, groups, trial_x, h_panel, s_panel, pattern):
    own, rows, width = trial_x.shape
    depth = h_panel.shape[1]
    chunk = 256
    chunks = width // chunk
    stats = -(-len(stat_pairs(own, own * groups)) // 8) * 8
    dma = pltpu.SemaphoreType.DMA
    normal, facts = pl.pallas_call(
        functools.partial(body, domains, groups, chunk),
        out_shape=(jax.ShapeDtypeStruct(trial_x.shape, F32), jax.ShapeDtypeStruct((2 * own,), F32)),
        in_specs=[pl.BlockSpec(memory_space=pltpu.HBM)] * 4,
        out_specs=(pl.BlockSpec(memory_space=pltpu.VMEM), pl.BlockSpec(memory_space=pltpu.SMEM)),
        scratch_shapes=[
            pltpu.SMEM(pattern.shape, jnp.int32),
            pltpu.VMEM((own, 3 * rows, width), BF16),
            pltpu.VMEM((groups - 1, own, rows, width), BF16),
            pltpu.VMEM((rows, depth), BF16),
            pltpu.VMEM((rows, depth), BF16),
            pltpu.VMEM((depth, 3 * rows), BF16),
            pltpu.VMEM((2 * rows, 3 * rows), BF16),
            pltpu.VMEM((own, 2 * rows, width), F32),
            pltpu.VMEM((stats, 8, 128), F32),
            pltpu.VMEM((domains, -(-stats // 128), 128), F32),
            pltpu.VMEM((domains, own, 128), F32),
            dma((4,)),
            dma((2, chunks)), dma((2, chunks)),
            dma((groups - 1, chunks)), dma((groups - 1, chunks)),
            dma((domains,)), dma((domains,)), dma((domains,)), dma((domains,)),
        ],
        compiler_params=pltpu.CompilerParams(
            collective_id=0, has_side_effects=True, vmem_limit_bytes=40 * 1024 * 1024),
    )(*[pltpu.with_memory_space_constraint(v, pltpu.HBM) for v in (pattern, trial_x, h_panel, s_panel)])
    theta, mean_sq = facts[:own], facts[own:]
    scaled = normal * lax.rsqrt(mean_sq + 1e-06)[:, None, None]
    return theta, scaled.astype(BF16), mean_sq


def solution(mesh):
    in_specs = (P("trial", "space", None), P("space", None), P("space", None), P("space", None))
    out_specs = (P("trial"), P("trial", "space", None), P("trial"))
    return jax.shard_map(
        functools.partial(on_device, mesh.shape["space"], mesh.shape["trial"]),
        mesh=mesh, in_specs=in_specs, out_specs=out_specs, check_vma=False
    )
```

```python
import functools

import jax
import jax.numpy as jnp
from jax import lax
from jax.experimental import pallas as pl
from jax.experimental.pallas import tpu as pltpu
from jax.sharding import PartitionSpec as P

F32, BF16 = jnp.float32, jnp.bfloat16
GROUP = 30


def stat_pairs(own, states):
    pairs = [(("s", k), ("h", k)) for k in range(own)]
    pairs += [(("s", k), ("s", k)) for k in range(own)]
    pairs += [(("x", t), ("h", k)) for t in range(states) for k in range(own)]
    pairs += [(("x", t), ("s", k)) for t in range(states) for k in range(own)]
    pairs += [(("x", t), ("x", u)) for t in range(states) for u in range(t + 1)]
    return pairs


def cholesky_solve(gram, rhs):
    n = len(rhs)
    low = [[None] * n for _ in range(n)]
    inv = [None] * n
    for j in range(n):
        d = gram[j][j]
        for k in range(j):
            d = d - low[j][k] * low[j][k]
        inv[j] = 1.0 / jnp.sqrt(d)
        for i in range(j + 1, n):
            v = gram[i][j]
            for k in range(j):
                v = v - low[i][k] * low[j][k]
            low[i][j] = v * inv[j]
    out = []
    for col in range(len(rhs[0])):
        y = []
        for i in range(n):
            v = rhs[i][col]
            for k in range(i):
                v = v - low[i][k] * y[k]
            y.append(v * inv[i])
        z = [None] * n
        for i in reversed(range(n)):
            v = y[i]
            for k in range(i + 1, n):
                v = v - low[k][i] * z[k]
            z[i] = v * inv[i]
        out.append(z)
    return out


def body(domains, groups, inner, chunk, pat_hbm, x, h, s, out, facts,
         pat, ext, oth, hp, sp, pick, hext, img, acc, slots, nslots,
         lsem, nb_send, nb_recv, tr_send, tr_recv, st_send, st_recv, nm_send, nm_recv, ready):
    own, rows, width = x.shape
    atoms_dev, nslot = pat.shape
    block = rows // atoms_dev
    atoms = atoms_dev * domains
    span = 3 * rows
    states = own * groups
    chunks = width // chunk
    me, mt = lax.axis_index("space"), lax.axis_index("trial")
    right, left = lax.rem(me + 1, domains), lax.rem(me + domains - 1, domains)

    loads = [
        pltpu.make_async_copy(x, ext.at[:, pl.ds(rows, rows), :], lsem.at[0]),
        pltpu.make_async_copy(h, hp, lsem.at[1]),
        pltpu.make_async_copy(s, sp, lsem.at[2]),
        pltpu.make_async_copy(pat_hbm, pat, lsem.at[3]),
    ]
    for load in loads:
        load.start()

    barrier = pltpu.get_barrier_semaphore()

    outer = domains // inner
    spot_in, spot_out = lax.rem(me, inner), me // inner
    first_in = me - spot_in
    friends = [right, left]
    friends += [first_in + lax.rem(spot_in + k, inner) for k in range(1, inner)]
    friends += [spot_in + inner * lax.rem(spot_out + k, outer) for k in range(1, outer)]
    for friend in friends:
        pl.semaphore_signal(barrier, inc=1, device_id={"space": friend})
    for k in range(1, groups):
        pl.semaphore_signal(barrier, inc=1, device_id={"trial": lax.rem(mt + k, groups)})
    pl.semaphore_wait(barrier, len(friends) + groups - 1)

    def neighbour_copy(side, c):
        cols = pl.ds(pl.multiple_of(c * chunk, chunk), chunk)
        return pltpu.make_async_remote_copy(
            src_ref=x.at[:, :, cols],
            dst_ref=ext.at[:, pl.ds(2 * rows * side, rows), cols],
            send_sem=nb_send.at[side, c], recv_sem=nb_recv.at[side, c],
            device_id={"space": left if side else right})

    def trial_copy(k, c):
        cols = pl.ds(pl.multiple_of(c * chunk, chunk), chunk)
        return pltpu.make_async_remote_copy(
            src_ref=x.at[:, :, cols], dst_ref=oth.at[k - 1, :, :, cols],
            send_sem=tr_send.at[k - 1, c], recv_sem=tr_recv.at[k - 1, c],
            device_id={"trial": lax.rem(mt + k, groups)})

    def arrivals(c):
        return [neighbour_copy(0, c), neighbour_copy(1, c)] + [trial_copy(k, c) for k in range(1, groups)]

    for c in range(chunks):
        for copy in arrivals(c):
            copy.start()

    vouched = [spot_in + inner * lax.rem(spot_out + k, outer) for k in range(1, outer)]
    for friend in vouched:
        pl.semaphore_signal(ready, inc=1, device_id={"space": friend})
    pl.semaphore_wait(ready, outer - 1)
    peers = [lax.rem(spot_out + ko, outer) * inner + lax.rem(spot_in + ki, inner)
             for ko in list(range(1, outer)) + [0] for ki in range(inner) if ko or ki]

    acc[...] = jnp.zeros_like(acc)
    loads[1].wait()
    loads[2].wait()
    loads[3].wait()
    diff = (lax.broadcasted_iota(jnp.int32, (block, span), 1)
            - lax.broadcasted_iota(jnp.int32, (block, span), 0))

    def densify(a, carry):
        for b in range(nslot):
            link = lax.rem(pat[a, b] - me * atoms_dev + atoms_dev + atoms, atoms)
            pick[b * block:(b + 1) * block, :] = jnp.where(diff == link * block, 1.0, 0.0).astype(BF16)
        at = pl.multiple_of(a * block, block)
        ha = jnp.dot(hp[pl.ds(at, block), :], pick[...], preferred_element_type=F32)
        hext[pl.ds(at, block), :] = ha.astype(BF16)
        sa = jnp.dot(sp[pl.ds(at, block), :], pick[...], preferred_element_type=F32)
        hext[pl.ds(pl.multiple_of(rows + a * block, block), block), :] = sa.astype(BF16)
        return carry
    lax.fori_loop(0, atoms_dev, densify, 0)
    loads[0].wait()

    pairs = stat_pairs(own, states)

    def fetch(name, at, col):
        kind, k = name
        cols = pl.ds(pl.multiple_of(col, 128), 128)
        if kind == "h":
            return img[k, pl.ds(at, 16), cols]
        if kind == "s":
            return img[k, pl.ds(pl.multiple_of(rows + at, 16), 16), cols]
        if k < own:
            return ext[k, pl.ds(pl.multiple_of(rows + at, 16), 16), cols].astype(F32)
        return oth[k // own - 1, k % own, pl.ds(at, 16), cols].astype(F32)

    def on_chunk(c, carry):
        for copy in arrivals(c):
            copy.wait_recv()
        cols = pl.ds(pl.multiple_of(c * chunk, chunk), chunk)
        for k in range(own):
            img[k, :, cols] = jnp.dot(hext[...], ext[k, :, cols], preferred_element_type=F32)
        for first in range(0, len(pairs), GROUP):
            part = pairs[first:first + GROUP]

            def on_rows(r, sums):
                at = pl.multiple_of(r * 16, 16)
                for piece in range(chunk // 128):
                    have = {}
                    new = []
                    for (a, b), total in zip(part, sums):
                        for name in (a, b):
                            if name not in have:
                                have[name] = fetch(name, at, c * chunk + piece * 128)
                        p = have[a] * have[b]
                        new.append(total + (p[:8] + p[8:]))
                    sums = tuple(new)
                return sums
            zero = jnp.zeros((8, 128), F32)
            sums = lax.fori_loop(0, rows // 16, on_rows, (zero,) * len(part))
            for i, v in enumerate(sums):
                acc[first + i] += v
        return carry
    lax.fori_loop(0, chunks, on_chunk, 0)

    lines = slots.shape[1]
    spot = (lax.broadcasted_iota(jnp.int32, (8, 128), 1)
            - lax.broadcasted_iota(jnp.int32, (8, 128), 0))
    for line in range(lines):
        message = jnp.zeros((8, 128), F32)
        for g in range(16 * line, min(16 * line + 16, acc.shape[0] // 8)):
            ends = jnp.sum(jnp.sum(acc[g * 8:(g + 1) * 8], axis=1), axis=1, keepdims=True)
            message = jnp.where(spot == (g % 16) * 8, jnp.broadcast_to(ends, (8, 128)), message)
        slots[me, line:line + 1] = jnp.sum(message, axis=0, keepdims=True)

    unsent = []

    def share(buffer, send, recv):
        def copy(k, place, to):
            return pltpu.make_async_remote_copy(
                src_ref=buffer.at[place], dst_ref=buffer.at[place],
                send_sem=send.at[k], recv_sem=recv.at[place], device_id={"space": to})
        for k, peer in enumerate(peers):
            away = copy(k, me, peer)
            away.start()
            unsent.append(away)
        for k, peer in enumerate(peers):
            copy(k, peer, peer).wait_recv()
        result = buffer[0]
        for d in range(1, domains):
            result = result + buffer[d]
        return result

    total = share(slots, st_send, st_recv)
    value = {}
    for i, name in enumerate(pairs):
        value[name] = jnp.broadcast_to(total[i // 128:i // 128 + 1, i % 128:i % 128 + 1], (8, 128))
    theta = [value[("s", k), ("h", k)] / (value[("s", k), ("s", k)] + 1e-06) for k in range(own)]
    corr = [[value[("x", t), ("h", k)] - theta[k] * value[("x", t), ("s", k)] for k in range(own)]
            for t in range(states)]
    gram = [[value[("x", t), ("x", u)] for u in range(t + 1)] for t in range(states)]
    coeffs = cholesky_solve(gram, corr)
    for k in range(own):
        facts[k] = theta[k][0, 0]

    def wide(v):
        return jnp.concatenate([v, v], axis=0)

    zero = jnp.zeros((8, 128), F32)

    def on_normal(r, sums):
        at = pl.multiple_of(r * 16, 16)
        sums = list(sums)
        for col in range(0, width, 128):
            xs = [fetch(("x", t), at, col) for t in range(states)]
            for k in range(own):
                n = fetch(("h", k), at, col) - wide(theta[k]) * fetch(("s", k), at, col)
                lump = wide(coeffs[k][0]) * xs[0]
                for t in range(1, states):
                    lump = lump + wide(coeffs[k][t]) * xs[t]
                n = n - lump
                out[k, pl.ds(at, 16), pl.ds(col, 128)] = n
                p = n * n
                sums[k] = sums[k] + (p[:8] + p[8:])
        return tuple(sums)
    sums = lax.fori_loop(0, rows // 16, on_normal, (zero,) * own)
    lane = lax.broadcasted_iota(jnp.int32, (1, 128), 1)
    packed = jnp.zeros((1, 128), F32)
    for k in range(own):
        line = jnp.sum(jnp.sum(sums[k], axis=0, keepdims=True), axis=1, keepdims=True)
        packed = jnp.where(lane == k, jnp.broadcast_to(line, (1, 128)), packed)
    nslots[me] = packed
    norm = share(nslots, nm_send, nm_recv)
    norm = norm / float(domains * rows * width)
    for k in range(own):
        facts[own + k] = norm[0, k]
    for c in range(chunks):
        for copy in arrivals(c):
            copy.wait_send()
    for copy in unsent:
        copy.wait_send()


def on_device(domains, groups, trial_x, h_panel, s_panel, pattern):
    own, rows, width = trial_x.shape
    depth = h_panel.shape[1]
    chunk = 256
    chunks = width // chunk
    stats = -(-len(stat_pairs(own, own * groups)) // 8) * 8
    dma = pltpu.SemaphoreType.DMA
    inner = max(d for d in range(1, domains + 1) if domains % d == 0 and d * d <= domains)
    outer = domains // inner
    normal, facts = pl.pallas_call(
        functools.partial(body, domains, groups, inner, chunk),
        out_shape=(jax.ShapeDtypeStruct(trial_x.shape, F32), jax.ShapeDtypeStruct((2 * own,), F32)),
        in_specs=[pl.BlockSpec(memory_space=pltpu.HBM)] * 4,
        out_specs=(pl.BlockSpec(memory_space=pltpu.VMEM), pl.BlockSpec(memory_space=pltpu.SMEM)),
        scratch_shapes=[
            pltpu.SMEM(pattern.shape, jnp.int32),
            pltpu.VMEM((own, 3 * rows, width), BF16),
            pltpu.VMEM((groups - 1, own, rows, width), BF16),
            pltpu.VMEM((rows, depth), BF16),
            pltpu.VMEM((rows, depth), BF16),
            pltpu.VMEM((depth, 3 * rows), BF16),
            pltpu.VMEM((2 * rows, 3 * rows), BF16),
            pltpu.VMEM((own, 2 * rows, width), F32),
            pltpu.VMEM((stats, 8, 128), F32),
            pltpu.VMEM((domains, -(-stats // 128), 128), F32),
            pltpu.VMEM((domains, 1, 128), F32),
            dma((4,)),
            dma((2, chunks)), dma((2, chunks)),
            dma((groups - 1, chunks)), dma((groups - 1, chunks)),
            dma((domains,)), dma((domains,)), dma((domains,)), dma((domains,)),
            pltpu.SemaphoreType.REGULAR,
        ],
        compiler_params=pltpu.CompilerParams(
            collective_id=0, has_side_effects=True, vmem_limit_bytes=40 * 1024 * 1024),
    )(*[pltpu.with_memory_space_constraint(v, pltpu.HBM) for v in (pattern, trial_x, h_panel, s_panel)])
    theta, mean_sq = facts[:own], facts[own:]
    scaled = normal * lax.rsqrt(mean_sq + 1e-06)[:, None, None]
    return theta, scaled.astype(BF16), mean_sq


def solution(mesh):
    in_specs = (P("trial", "space", None), P("space", None), P("space", None), P("space", None))
    out_specs = (P("trial"), P("trial", "space", None), P("trial"))
    return jax.shard_map(
        functools.partial(on_device, mesh.shape["space"], mesh.shape["trial"]),
        mesh=mesh, in_specs=in_specs, out_specs=out_specs, check_vma=False
    )
```

```python
import functools

import jax
import jax.numpy as jnp
from jax import lax
from jax.experimental import pallas as pl
from jax.experimental.pallas import tpu as pltpu
from jax.sharding import PartitionSpec as P

F32, BF16 = jnp.float32, jnp.bfloat16
GROUP = 30


def stat_pairs(own, states):
    pairs = [(("s", k), ("h", k)) for k in range(own)]
    pairs += [(("s", k), ("s", k)) for k in range(own)]
    pairs += [(("x", t), ("h", k)) for t in range(states) for k in range(own)]
    pairs += [(("x", t), ("s", k)) for t in range(states) for k in range(own)]
    pairs += [(("x", t), ("x", u)) for t in range(states) for u in range(t + 1)]
    return pairs


def cholesky_solve(gram, rhs):
    n = len(rhs)
    low = [[None] * n for _ in range(n)]
    inv = [None] * n
    for j in range(n):
        d = gram[j][j]
        for k in range(j):
            d = d - low[j][k] * low[j][k]
        inv[j] = 1.0 / jnp.sqrt(d)
        for i in range(j + 1, n):
            v = gram[i][j]
            for k in range(j):
                v = v - low[i][k] * low[j][k]
            low[i][j] = v * inv[j]
    out = []
    for col in range(len(rhs[0])):
        y = []
        for i in range(n):
            v = rhs[i][col]
            for k in range(i):
                v = v - low[i][k] * y[k]
            y.append(v * inv[i])
        z = [None] * n
        for i in reversed(range(n)):
            v = y[i]
            for k in range(i + 1, n):
                v = v - low[k][i] * z[k]
            z[i] = v * inv[i]
        out.append(z)
    return out


def body(domains, groups, inner, chunk, pat_hbm, x, h, s, out, facts,
         pat, ext, oth, hp, sp, pick, hext, img, acc, slots, nslots,
         lsem, nb_send, nb_recv, tr_send, tr_recv, st_send, st_recv, nm_send, nm_recv, ready):
    own, rows, width = x.shape
    atoms_dev, nslot = pat.shape
    block = rows // atoms_dev
    atoms = atoms_dev * domains
    span = 3 * rows
    states = own * groups
    chunks = width // chunk
    me, mt = lax.axis_index("space"), lax.axis_index("trial")
    right, left = lax.rem(me + 1, domains), lax.rem(me + domains - 1, domains)

    loads = [
        pltpu.make_async_copy(x, ext.at[:, pl.ds(rows, rows), :], lsem.at[0]),
        pltpu.make_async_copy(h, hp, lsem.at[1]),
        pltpu.make_async_copy(s, sp, lsem.at[2]),
        pltpu.make_async_copy(pat_hbm, pat, lsem.at[3]),
    ]
    for load in loads:
        load.start()

    barrier = pltpu.get_barrier_semaphore()

    outer = domains // inner
    spot_in, spot_out = lax.rem(me, inner), me // inner
    first_in = me - spot_in
    friends = [right, left]
    friends += [first_in + lax.rem(spot_in + k, inner) for k in range(1, inner)]
    friends += [spot_in + inner * lax.rem(spot_out + k, outer) for k in range(1, outer)]
    for friend in friends:
        pl.semaphore_signal(barrier, inc=1, device_id={"space": friend})
    for k in range(1, groups):
        pl.semaphore_signal(barrier, inc=1, device_id={"trial": lax.rem(mt + k, groups)})
    pl.semaphore_wait(barrier, len(friends) + groups - 1)

    def neighbour_copy(side, c):
        cols = pl.ds(pl.multiple_of(c * chunk, chunk), chunk)
        return pltpu.make_async_remote_copy(
            src_ref=x.at[:, :, cols],
            dst_ref=ext.at[:, pl.ds(2 * rows * side, rows), cols],
            send_sem=nb_send.at[side, c], recv_sem=nb_recv.at[side, c],
            device_id={"space": left if side else right})

    def trial_copy(k, c):
        cols = pl.ds(pl.multiple_of(c * chunk, chunk), chunk)
        return pltpu.make_async_remote_copy(
            src_ref=x.at[:, :, cols], dst_ref=oth.at[k - 1, :, :, cols],
            send_sem=tr_send.at[k - 1, c], recv_sem=tr_recv.at[k - 1, c],
            device_id={"trial": lax.rem(mt + k, groups)})

    def arrivals(c):
        return [neighbour_copy(0, c), neighbour_copy(1, c)] + [trial_copy(k, c) for k in range(1, groups)]

    for c in range(chunks):
        for copy in arrivals(c):
            copy.start()

    vouched = [spot_in + inner * lax.rem(spot_out + k, outer) for k in range(1, outer)]
    for friend in vouched:
        pl.semaphore_signal(ready, inc=1, device_id={"space": friend})
    pl.semaphore_wait(ready, outer - 1)
    peers = [lax.rem(spot_out + ko, outer) * inner + lax.rem(spot_in + ki, inner)
             for ko in list(range(1, outer)) + [0] for ki in range(inner) if ko or ki]

    acc[...] = jnp.zeros_like(acc)
    loads[1].wait()
    loads[2].wait()
    loads[3].wait()
    diff = (lax.broadcasted_iota(jnp.int32, (block, span), 1)
            - lax.broadcasted_iota(jnp.int32, (block, span), 0))

    def densify(a, carry):
        for b in range(nslot):
            link = lax.rem(pat[a, b] - me * atoms_dev + atoms_dev + atoms, atoms)
            pick[b * block:(b + 1) * block, :] = jnp.where(diff == link * block, 1.0, 0.0).astype(BF16)
        at = pl.multiple_of(a * block, block)
        ha = jnp.dot(hp[pl.ds(at, block), :], pick[...], preferred_element_type=F32)
        hext[pl.ds(at, block), :] = ha.astype(BF16)
        sa = jnp.dot(sp[pl.ds(at, block), :], pick[...], preferred_element_type=F32)
        hext[pl.ds(pl.multiple_of(rows + a * block, block), block), :] = sa.astype(BF16)
        return carry
    lax.fori_loop(0, atoms_dev, densify, 0)
    loads[0].wait()

    pairs = stat_pairs(own, states)

    def fetch(name, at, col):
        kind, k = name
        cols = pl.ds(pl.multiple_of(col, 128), 128)
        if kind == "h":
            return img[k, pl.ds(at, 16), cols]
        if kind == "s":
            return img[k, pl.ds(pl.multiple_of(rows + at, 16), 16), cols]
        if k < own:
            return ext[k, pl.ds(pl.multiple_of(rows + at, 16), 16), cols].astype(F32)
        return oth[k // own - 1, k % own, pl.ds(at, 16), cols].astype(F32)

    def on_chunk(c, carry):
        for copy in arrivals(c):
            copy.wait_recv()
        cols = pl.ds(pl.multiple_of(c * chunk, chunk), chunk)
        for k in range(own):
            img[k, :, cols] = jnp.dot(hext[...], ext[k, :, cols], preferred_element_type=F32)
        for first in range(0, len(pairs), GROUP):
            part = pairs[first:first + GROUP]

            def on_rows(r, sums):
                at = pl.multiple_of(r * 16, 16)
                for piece in range(chunk // 128):
                    have = {}
                    new = []
                    for (a, b), total in zip(part, sums):
                        for name in (a, b):
                            if name not in have:
                                have[name] = fetch(name, at, c * chunk + piece * 128)
                        p = have[a] * have[b]
                        new.append(total + (p[:8] + p[8:]))
                    sums = tuple(new)
                return sums
            zero = jnp.zeros((8, 128), F32)
            sums = lax.fori_loop(0, rows // 16, on_rows, (zero,) * len(part))
            for i, v in enumerate(sums):
                acc[first + i] += v
        return carry
    lax.fori_loop(0, chunks, on_chunk, 0)

    lines = slots.shape[1]
    spot = (lax.broadcasted_iota(jnp.int32, (8, 128), 1)
            - lax.broadcasted_iota(jnp.int32, (8, 128), 0))
    for line in range(lines):
        message = jnp.zeros((8, 128), F32)
        for g in range(16 * line, min(16 * line + 16, acc.shape[0] // 8)):
            ends = jnp.sum(jnp.sum(acc[g * 8:(g + 1) * 8], axis=1), axis=1, keepdims=True)
            message = jnp.where(spot == (g % 16) * 8, jnp.broadcast_to(ends, (8, 128)), message)
        slots[me, line:line + 1] = jnp.sum(message, axis=0, keepdims=True)

    def share(buffer, send, recv, meanwhile):
        def copy(place, to):
            return pltpu.make_async_remote_copy(
                src_ref=buffer.at[place], dst_ref=buffer.at[place],
                send_sem=send, recv_sem=recv, device_id={"space": to})
        for peer in peers:
            copy(me, peer).start()
        meanwhile()
        every = copy(pl.ds(0, domains - 1), right)
        every.wait_recv()
        result = buffer[0]
        for d in range(1, domains):
            result = result + buffer[d]
        return result, every.wait_send

    def bulk_gone():
        for c in range(chunks):
            for copy in arrivals(c):
                copy.wait_send()

    total, stats_gone = share(slots, st_send, st_recv, bulk_gone)
    value = {}
    for i, name in enumerate(pairs):
        value[name] = jnp.broadcast_to(total[i // 128:i // 128 + 1, i % 128:i % 128 + 1], (8, 128))
    theta = [value[("s", k), ("h", k)] / (value[("s", k), ("s", k)] + 1e-06) for k in range(own)]
    corr = [[value[("x", t), ("h", k)] - theta[k] * value[("x", t), ("s", k)] for k in range(own)]
            for t in range(states)]
    gram = [[value[("x", t), ("x", u)] for u in range(t + 1)] for t in range(states)]
    coeffs = cholesky_solve(gram, corr)
    for k in range(own):
        facts[k] = theta[k][0, 0]

    def wide(v):
        return jnp.concatenate([v, v], axis=0)

    zero = jnp.zeros((8, 128), F32)

    def on_normal(r, sums):
        at = pl.multiple_of(r * 16, 16)
        sums = list(sums)
        for col in range(0, width, 128):
            xs = [fetch(("x", t), at, col) for t in range(states)]
            for k in range(own):
                n = fetch(("h", k), at, col) - wide(theta[k]) * fetch(("s", k), at, col)
                lump = wide(coeffs[k][0]) * xs[0]
                for t in range(1, states):
                    lump = lump + wide(coeffs[k][t]) * xs[t]
                n = n - lump
                out[k, pl.ds(at, 16), pl.ds(col, 128)] = n
                p = n * n
                sums[k] = sums[k] + (p[:8] + p[8:])
        return tuple(sums)
    sums = lax.fori_loop(0, rows // 16, on_normal, (zero,) * own)
    lane = lax.broadcasted_iota(jnp.int32, (1, 128), 1)
    packed = jnp.zeros((1, 128), F32)
    for k in range(own):
        line = jnp.sum(jnp.sum(sums[k], axis=0, keepdims=True), axis=1, keepdims=True)
        packed = jnp.where(lane == k, jnp.broadcast_to(line, (1, 128)), packed)
    nslots[me] = packed
    norm, norms_gone = share(nslots, nm_send, nm_recv, stats_gone)
    norm = norm / float(domains * rows * width)
    for k in range(own):
        facts[own + k] = norm[0, k]
    norms_gone()


def on_device(domains, groups, trial_x, h_panel, s_panel, pattern):
    own, rows, width = trial_x.shape
    depth = h_panel.shape[1]
    chunk = 256
    chunks = width // chunk
    stats = -(-len(stat_pairs(own, own * groups)) // 8) * 8
    dma = pltpu.SemaphoreType.DMA
    inner = max(d for d in range(1, domains + 1) if domains % d == 0 and d * d <= domains)
    outer = domains // inner
    normal, facts = pl.pallas_call(
        functools.partial(body, domains, groups, inner, chunk),
        out_shape=(jax.ShapeDtypeStruct(trial_x.shape, F32), jax.ShapeDtypeStruct((2 * own,), F32)),
        in_specs=[pl.BlockSpec(memory_space=pltpu.HBM)] * 4,
        out_specs=(pl.BlockSpec(memory_space=pltpu.VMEM), pl.BlockSpec(memory_space=pltpu.SMEM)),
        scratch_shapes=[
            pltpu.SMEM(pattern.shape, jnp.int32),
            pltpu.VMEM((own, 3 * rows, width), BF16),
            pltpu.VMEM((groups - 1, own, rows, width), BF16),
            pltpu.VMEM((rows, depth), BF16),
            pltpu.VMEM((rows, depth), BF16),
            pltpu.VMEM((depth, 3 * rows), BF16),
            pltpu.VMEM((2 * rows, 3 * rows), BF16),
            pltpu.VMEM((own, 2 * rows, width), F32),
            pltpu.VMEM((stats, 8, 128), F32),
            pltpu.VMEM((domains, -(-stats // 128), 128), F32),
            pltpu.VMEM((domains, 1, 128), F32),
            dma((4,)),
            dma((2, chunks)), dma((2, chunks)),
            dma((groups - 1, chunks)), dma((groups - 1, chunks)),
            dma, dma, dma, dma,
            pltpu.SemaphoreType.REGULAR,
        ],
        compiler_params=pltpu.CompilerParams(
            collective_id=0, has_side_effects=True, vmem_limit_bytes=40 * 1024 * 1024),
    )(*[pltpu.with_memory_space_constraint(v, pltpu.HBM) for v in (pattern, trial_x, h_panel, s_panel)])
    theta, mean_sq = facts[:own], facts[own:]
    scaled = normal * lax.rsqrt(mean_sq + 1e-06)[:, None, None]
    return theta, scaled.astype(BF16), mean_sq


def solution(mesh):
    in_specs = (P("trial", "space", None), P("space", None), P("space", None), P("space", None))
    out_specs = (P("trial"), P("trial", "space", None), P("trial"))
    return jax.shard_map(
        functools.partial(on_device, mesh.shape["space"], mesh.shape["trial"]),
        mesh=mesh, in_specs=in_specs, out_specs=out_specs, check_vma=False
    )
```

```python
import functools

import jax
import jax.numpy as jnp
from jax import lax
from jax.experimental import pallas as pl
from jax.experimental.pallas import tpu as pltpu
from jax.sharding import PartitionSpec as P

F32, BF16 = jnp.float32, jnp.bfloat16
GROUP = 30


def stat_pairs(own, states):
    pairs = [(("s", k), ("h", k)) for k in range(own)]
    pairs += [(("s", k), ("s", k)) for k in range(own)]
    pairs += [(("x", t), ("h", k)) for t in range(states) for k in range(own)]
    pairs += [(("x", t), ("s", k)) for t in range(states) for k in range(own)]
    pairs += [(("x", t), ("x", u)) for t in range(states) for u in range(t + 1)]
    return pairs


def cholesky_solve(gram, rhs):
    n = len(rhs)
    low = [[None] * n for _ in range(n)]
    inv = [None] * n
    for j in range(n):
        d = gram[j][j]
        for k in range(j):
            d = d - low[j][k] * low[j][k]
        inv[j] = 1.0 / jnp.sqrt(d)
        for i in range(j + 1, n):
            v = gram[i][j]
            for k in range(j):
                v = v - low[i][k] * low[j][k]
            low[i][j] = v * inv[j]
    out = []
    for col in range(len(rhs[0])):
        y = []
        for i in range(n):
            v = rhs[i][col]
            for k in range(i):
                v = v - low[i][k] * y[k]
            y.append(v * inv[i])
        z = [None] * n
        for i in reversed(range(n)):
            v = y[i]
            for k in range(i + 1, n):
                v = v - low[k][i] * z[k]
            z[i] = v * inv[i]
        out.append(z)
    return out


def body(domains, groups, inner, chunk, pat_hbm, x, h, s, out, facts,
         pat, ext, oth, hp, sp, pick, hext, img, acc, slots, nslots,
         lsem, nb_send, nb_recv, tr_send, tr_recv, st_send, st_recv, nm_send, nm_recv, ready):
    own, rows, width = x.shape
    atoms_dev, nslot = pat.shape
    block = rows // atoms_dev
    atoms = atoms_dev * domains
    span = 3 * rows
    states = own * groups
    chunks = width // chunk
    me, mt = lax.axis_index("space"), lax.axis_index("trial")
    right, left = lax.rem(me + 1, domains), lax.rem(me + domains - 1, domains)

    loads = [
        pltpu.make_async_copy(x, ext.at[:, pl.ds(rows, rows), :], lsem.at[0]),
        pltpu.make_async_copy(h, hp, lsem.at[1]),
        pltpu.make_async_copy(s, sp, lsem.at[2]),
        pltpu.make_async_copy(pat_hbm, pat, lsem.at[3]),
    ]
    for load in loads:
        load.start()

    barrier = pltpu.get_barrier_semaphore()

    outer = domains // inner
    spot_in, spot_out = lax.rem(me, inner), me // inner
    first_in = me - spot_in
    friends = [right, left]
    friends += [first_in + lax.rem(spot_in + k, inner) for k in range(1, inner)]
    friends += [spot_in + inner * lax.rem(spot_out + k, outer) for k in range(1, outer)]
    for friend in friends:
        pl.semaphore_signal(barrier, inc=1, device_id={"space": friend})
    for k in range(1, groups):
        pl.semaphore_signal(barrier, inc=1, device_id={"trial": lax.rem(mt + k, groups)})
    pl.semaphore_wait(barrier, len(friends) + groups - 1)

    def neighbour_copy(side, c):
        cols = pl.ds(pl.multiple_of(c * chunk, chunk), chunk)
        return pltpu.make_async_remote_copy(
            src_ref=x.at[:, :, cols],
            dst_ref=ext.at[:, pl.ds(2 * rows * side, rows), cols],
            send_sem=nb_send.at[side, c], recv_sem=nb_recv.at[side, c],
            device_id={"space": left if side else right})

    def trial_copy(k, c):
        cols = pl.ds(pl.multiple_of(c * chunk, chunk), chunk)
        return pltpu.make_async_remote_copy(
            src_ref=x.at[:, :, cols], dst_ref=oth.at[k - 1, :, :, cols],
            send_sem=tr_send.at[k - 1, c], recv_sem=tr_recv.at[k - 1, c],
            device_id={"trial": lax.rem(mt + k, groups)})

    def arrivals(c):
        return [trial_copy(k, c) for k in range(1, groups)] + [neighbour_copy(0, c), neighbour_copy(1, c)]

    for c in range(chunks):
        for copy in arrivals(c):
            copy.start()

    vouched = [spot_in + inner * lax.rem(spot_out + k, outer) for k in range(1, outer)]
    for friend in vouched:
        pl.semaphore_signal(ready, inc=1, device_id={"space": friend})
    pl.semaphore_wait(ready, outer - 1)
    peers = [lax.rem(spot_out + ko, outer) * inner + lax.rem(spot_in + ki, inner)
             for ko in list(range(1, outer)) + [0] for ki in range(inner) if ko or ki]

    acc[...] = jnp.zeros_like(acc)
    loads[1].wait()
    loads[2].wait()
    loads[3].wait()
    diff = (lax.broadcasted_iota(jnp.int32, (block, span), 1)
            - lax.broadcasted_iota(jnp.int32, (block, span), 0))

    def densify(a, carry):
        for b in range(nslot):
            link = lax.rem(pat[a, b] - me * atoms_dev + atoms_dev + atoms, atoms)
            pick[b * block:(b + 1) * block, :] = jnp.where(diff == link * block, 1.0, 0.0).astype(BF16)
        at = pl.multiple_of(a * block, block)
        ha = jnp.dot(hp[pl.ds(at, block), :], pick[...], preferred_element_type=F32)
        hext[pl.ds(at, block), :] = ha.astype(BF16)
        sa = jnp.dot(sp[pl.ds(at, block), :], pick[...], preferred_element_type=F32)
        hext[pl.ds(pl.multiple_of(rows + a * block, block), block), :] = sa.astype(BF16)
        return carry
    lax.fori_loop(0, atoms_dev, densify, 0)
    loads[0].wait()

    pairs = stat_pairs(own, states)

    def fetch(name, at, col):
        kind, k = name
        cols = pl.ds(pl.multiple_of(col, 128), 128)
        if kind == "h":
            return img[k, pl.ds(at, 16), cols]
        if kind == "s":
            return img[k, pl.ds(pl.multiple_of(rows + at, 16), 16), cols]
        if k < own:
            return ext[k, pl.ds(pl.multiple_of(rows + at, 16), 16), cols].astype(F32)
        return oth[k // own - 1, k % own, pl.ds(at, 16), cols].astype(F32)

    def on_chunk(c, carry):
        for copy in arrivals(c):
            copy.wait_recv()
        cols = pl.ds(pl.multiple_of(c * chunk, chunk), chunk)
        for k in range(own):
            img[k, :, cols] = jnp.dot(hext[...], ext[k, :, cols], preferred_element_type=F32)
        for first in range(0, len(pairs), GROUP):
            part = pairs[first:first + GROUP]

            def on_rows(r, sums):
                at = pl.multiple_of(r * 16, 16)
                for piece in range(chunk // 128):
                    have = {}
                    new = []
                    for (a, b), total in zip(part, sums):
                        for name in (a, b):
                            if name not in have:
                                have[name] = fetch(name, at, c * chunk + piece * 128)
                        p = have[a] * have[b]
                        new.append(total + (p[:8] + p[8:]))
                    sums = tuple(new)
                return sums
            zero = jnp.zeros((8, 128), F32)
            sums = lax.fori_loop(0, rows // 16, on_rows, (zero,) * len(part))
            for i, v in enumerate(sums):
                acc[first + i] += v
        return carry
    lax.fori_loop(0, chunks, on_chunk, 0)

    lines = slots.shape[1]
    spot = (lax.broadcasted_iota(jnp.int32, (8, 128), 1)
            - lax.broadcasted_iota(jnp.int32, (8, 128), 0))
    for line in range(lines):
        message = jnp.zeros((8, 128), F32)
        for g in range(16 * line, min(16 * line + 16, acc.shape[0] // 8)):
            ends = jnp.sum(jnp.sum(acc[g * 8:(g + 1) * 8], axis=1), axis=1, keepdims=True)
            message = jnp.where(spot == (g % 16) * 8, jnp.broadcast_to(ends, (8, 128)), message)
        slots[me, line:line + 1] = jnp.sum(message, axis=0, keepdims=True)

    def share(buffer, send, recv, meanwhile):
        def copy(place, to):
            return pltpu.make_async_remote_copy(
                src_ref=buffer.at[place], dst_ref=buffer.at[place],
                send_sem=send, recv_sem=recv, device_id={"space": to})
        for peer in peers:
            copy(me, peer).start()
        meanwhile()
        every = copy(pl.ds(0, domains - 1), right)
        every.wait_recv()
        result = buffer[0]
        for d in range(1, domains):
            result = result + buffer[d]
        return result, every.wait_send

    def bulk_gone():
        for c in range(chunks):
            for copy in arrivals(c):
                copy.wait_send()

    total, stats_gone = share(slots, st_send, st_recv, bulk_gone)
    value = {}
    for i, name in enumerate(pairs):
        value[name] = jnp.broadcast_to(total[i // 128:i // 128 + 1, i % 128:i % 128 + 1], (8, 128))
    theta = [value[("s", k), ("h", k)] / (value[("s", k), ("s", k)] + 1e-06) for k in range(own)]
    corr = [[value[("x", t), ("h", k)] - theta[k] * value[("x", t), ("s", k)] for k in range(own)]
            for t in range(states)]
    gram = [[value[("x", t), ("x", u)] for u in range(t + 1)] for t in range(states)]
    coeffs = cholesky_solve(gram, corr)
    for k in range(own):
        facts[k] = theta[k][0, 0]

    def wide(v):
        return jnp.concatenate([v, v], axis=0)

    zero = jnp.zeros((8, 128), F32)

    def on_normal(r, sums):
        at = pl.multiple_of(r * 16, 16)
        sums = list(sums)
        for col in range(0, width, 128):
            xs = [fetch(("x", t), at, col) for t in range(states)]
            for k in range(own):
                n = fetch(("h", k), at, col) - wide(theta[k]) * fetch(("s", k), at, col)
                lump = wide(coeffs[k][0]) * xs[0]
                for t in range(1, states):
                    lump = lump + wide(coeffs[k][t]) * xs[t]
                n = n - lump
                out[k, pl.ds(at, 16), pl.ds(col, 128)] = n
                p = n * n
                sums[k] = sums[k] + (p[:8] + p[8:])
        return tuple(sums)
    sums = lax.fori_loop(0, rows // 16, on_normal, (zero,) * own)
    lane = lax.broadcasted_iota(jnp.int32, (1, 128), 1)
    packed = jnp.zeros((1, 128), F32)
    for k in range(own):
        line = jnp.sum(jnp.sum(sums[k], axis=0, keepdims=True), axis=1, keepdims=True)
        packed = jnp.where(lane == k, jnp.broadcast_to(line, (1, 128)), packed)
    nslots[me] = packed
    norm, norms_gone = share(nslots, nm_send, nm_recv, stats_gone)
    norm = norm / float(domains * rows * width)
    for k in range(own):
        facts[own + k] = norm[0, k]
    norms_gone()


def on_device(domains, groups, trial_x, h_panel, s_panel, pattern):
    own, rows, width = trial_x.shape
    depth = h_panel.shape[1]
    chunk = 128
    chunks = width // chunk
    stats = -(-len(stat_pairs(own, own * groups)) // 8) * 8
    dma = pltpu.SemaphoreType.DMA
    inner = max(d for d in range(1, domains + 1) if domains % d == 0 and d * d <= domains)
    outer = domains // inner
    normal, facts = pl.pallas_call(
        functools.partial(body, domains, groups, inner, chunk),
        out_shape=(jax.ShapeDtypeStruct(trial_x.shape, F32), jax.ShapeDtypeStruct((2 * own,), F32)),
        in_specs=[pl.BlockSpec(memory_space=pltpu.HBM)] * 4,
        out_specs=(pl.BlockSpec(memory_space=pltpu.VMEM), pl.BlockSpec(memory_space=pltpu.SMEM)),
        scratch_shapes=[
            pltpu.SMEM(pattern.shape, jnp.int32),
            pltpu.VMEM((own, 3 * rows, width), BF16),
            pltpu.VMEM((groups - 1, own, rows, width), BF16),
            pltpu.VMEM((rows, depth), BF16),
            pltpu.VMEM((rows, depth), BF16),
            pltpu.VMEM((depth, 3 * rows), BF16),
            pltpu.VMEM((2 * rows, 3 * rows), BF16),
            pltpu.VMEM((own, 2 * rows, width), F32),
            pltpu.VMEM((stats, 8, 128), F32),
            pltpu.VMEM((domains, -(-stats // 128), 128), F32),
            pltpu.VMEM((domains, 1, 128), F32),
            dma((4,)),
            dma((2, chunks)), dma((2, chunks)),
            dma((groups - 1, chunks)), dma((groups - 1, chunks)),
            dma, dma, dma, dma,
            pltpu.SemaphoreType.REGULAR,
        ],
        compiler_params=pltpu.CompilerParams(
            collective_id=0, has_side_effects=True, vmem_limit_bytes=40 * 1024 * 1024),
    )(*[pltpu.with_memory_space_constraint(v, pltpu.HBM) for v in (pattern, trial_x, h_panel, s_panel)])
    theta, mean_sq = facts[:own], facts[own:]
    scaled = normal * lax.rsqrt(mean_sq + 1e-06)[:, None, None]
    return theta, scaled.astype(BF16), mean_sq


def solution(mesh):
    in_specs = (P("trial", "space", None), P("space", None), P("space", None), P("space", None))
    out_specs = (P("trial"), P("trial", "space", None), P("trial"))
    return jax.shard_map(
        functools.partial(on_device, mesh.shape["space"], mesh.shape["trial"]),
        mesh=mesh, in_specs=in_specs, out_specs=out_specs, check_vma=False
    )
```
